32 devices in a mesh: mem: 8 (over z, y), band: 4 (over x, core).
Axes of the slice: x: 2, y: 2, z: 4, core: 2. Of those that a mesh axis runs over, the one named last changes fastest.
Arguments:
- ensemble: float32 [256, 256, 256], P('mem', 'band'), may hold values from -8 to 8
- column_operator: float32 [128, 128], replicated, may hold values from -0.5 to 0.5
- patch_order: int32 [4, 64], P('band'), may hold values from 0 to 63, as said below
- obs_index: int32 [4, 64, 512], P('band'), may hold values from 0 to 255
- obs_count: int32 [4, 64], P('band', 'mem'), may hold values from 1 to 512
- obs_values: float32 [4, 64, 512], P('band', 'mem'), may hold values from -8 to 8
- obs_precision: float32 [4, 64, 512], P('band', 'mem'), may hold values from 2 to 50
Outputs:
- analysis: float32 [256, 256, 256], P('mem', 'band')
- transform: float32 [4, 64, 256, 256], P('band', 'mem')
The draws below stay inside these ranges and needn't reach their ends.
Inputs may be any that keep to these rules, and one draw needn't show every extreme that they name: `patch_order`: each row is a permutation of 0 to 63.
All inputs are finite; a program needn't handle non-finite values.
Results may differ from the reference program's by a relative error of at most 0.0003.
Values sent between devices are 32-bit elements; how exact they have to be, the bound alone decides.
A program may use at most 64 MiB of HBM per device.

```python
import math
import jax
import jax.numpy as jnp
from jax import lax

K = 256
LEV = 128
NCH = 128
PCOLS = 2
OBS = 512
ITERS = 12
BAND_PATCHES = 64
NPATCH = 256
PC = 256
CAND = 256
N_BAND = 4


def draw_patch_order(key, part):
    keys = jax.random.split(jax.random.fold_in(key, 11), N_BAND)
    return jax.vmap(lambda single: jax.random.permutation(single, BAND_PATCHES))(keys).astype(jnp.int32)


def draw_obs_count(key, part):
    first, second, third = jax.random.split(jax.random.fold_in(key, 23), 3)
    total = N_BAND * BAND_PATCHES
    top_power = OBS.bit_length() - 1
    powers = jax.random.randint(first, (total,), 0, top_power).astype(jnp.int32)
    lowest = jnp.left_shift(jnp.ones((total,), jnp.int32), powers)
    counts = lowest + jax.random.randint(second, (total,), 0, lowest).astype(jnp.int32)
    spot = jax.random.randint(third, (), 0, total)
    places = jnp.arange(total, dtype=jnp.int32)
    counts = jnp.where(places == spot, OBS, counts)
    counts = jnp.where(places == (spot + 1) % total, 1, counts)
    return counts.reshape(N_BAND, BAND_PATCHES).astype(jnp.int32)


def touch_ends(drawn, key, low, high):
    longest = drawn.shape.index(max(drawn.shape))
    spots = []
    for shift in (0, 1):
        where = [jax.random.randint(jax.random.fold_in(key, axis), (), 0, length) for axis, length in enumerate(drawn.shape)]
        where[longest] = (where[longest] + shift) % drawn.shape[longest]
        spots.append(tuple(where))
    return drawn.at[spots[0]].set(low).at[spots[1]].set(high)


def steps_of(rng, dims, shards, smallest, top_value):
    def one(axis_at, shards_of):
        draws = jax.random.uniform(jax.random.fold_in(jax.random.fold_in(rng, 6), axis_at), (shards_of,), jnp.float32, smallest / len(shards), top_value / len(shards))
        return jnp.repeat(jnp.exp(draws), dims[axis_at] // shards_of).reshape((-1,) + (1,) * (len(dims) - axis_at - 1))

    loudness = one(*shards[0])
    for cut in shards[1:]:
        loudness = loudness * one(*cut)
    return loudness


def gaussian(key, shape, deviation, limit, pieces=(), kind=jnp.bfloat16):
    values = jax.random.normal(key, shape, jnp.float32) * deviation
    if len(pieces) > 0:
        values = steps_of(key, shape, pieces, -0.22, 0.18) * values
    return jnp.clip(values, min=-limit, max=limit).astype(kind)


def setup_inputs(seed: int = 0) -> dict:
    key_of = jax.random.split(jax.random.key(seed), 8)
    ensemble = gaussian(key_of[0], (K, NPATCH, PC), 2.5, 8.0, ((0, 8), (1, 4)), jnp.float32)
    column_operator = jnp.clip(jax.random.uniform(key_of[1], (LEV, NCH), jnp.float32, -0.5, 0.5), -0.5, 0.5)
    patch_order = draw_patch_order(jax.random.fold_in(key_of[7], 71), 0)
    obs_index = touch_ends(jax.random.randint(key_of[3], (N_BAND, BAND_PATCHES, OBS), 0, CAND), jax.random.fold_in(key_of[3], 1), 0, CAND - 1).astype(jnp.int32)
    obs_count = draw_obs_count(jax.random.fold_in(key_of[7], 71), 0)
    obs_values = gaussian(key_of[5], (N_BAND, BAND_PATCHES, OBS), 1.5, 8.0, ((0, 4), (1, 8)), jnp.float32)
    obs_precision = jnp.clip(jnp.exp(math.log(50.0) - 3.218876 * jax.random.uniform(key_of[6], (N_BAND, BAND_PATCHES, OBS), jnp.float32) ** steps_of(key_of[6], (N_BAND, BAND_PATCHES, OBS), ((0, 4), (1, 8)), -0.2, 0.2)), 2.0, 50.0)
    return {"ensemble": ensemble, "column_operator": column_operator, "patch_order": patch_order, "obs_index": obs_index, "obs_count": obs_count, "obs_values": obs_values, "obs_precision": obs_precision}


def analyse(members, column_operator, index, count, values, precision):
    highest = lax.Precision.HIGHEST
    rows = members.shape[0]
    channel_values = jnp.dot(members.reshape(rows * PCOLS, LEV), column_operator, precision=highest).reshape(rows, PCOLS * NCH)
    picks = jnp.broadcast_to(index[None, :], (rows, OBS))
    observed = jnp.take_along_axis(channel_values, picks, axis=1)
    live = (jnp.arange(OBS, dtype=jnp.int32) < count).astype(jnp.float32)
    obs_weight = precision * live
    state_mean = lax.optimization_barrier(jnp.mean(members, axis=0))
    state_pert = members - state_mean
    obs_mean = lax.optimization_barrier(jnp.mean(observed, axis=0))
    obs_pert = observed - obs_mean
    innov = (values - obs_mean) * obs_weight
    gram = jnp.dot(obs_pert * obs_weight, obs_pert.T, precision=highest)
    identity = jnp.eye(rows, dtype=jnp.float32)
    system = gram + (K - 1.0) * identity
    trace_value = jnp.trace(system)
    ymat = system / trace_value
    zmat = identity
    for sweep in range(ITERS):
        turn = 1.5 * identity - 0.5 * jnp.dot(zmat, ymat, precision=highest)
        ymat, zmat = (jnp.dot(ymat, turn, precision=highest), jnp.dot(turn, zmat, precision=highest))
    root = zmat / jnp.sqrt(trace_value)
    spread = math.sqrt(K - 1.0) * root
    projected = jnp.dot(obs_pert, innov, precision=highest)
    mean_weight = jnp.dot(root, jnp.dot(root, projected, precision=highest), precision=highest)
    coef = spread + mean_weight[:, None]
    result = state_mean + jnp.dot(coef.T, state_pert, precision=highest)
    return (spread, result)

def reference(ensemble, column_operator, patch_order, obs_index, obs_count, obs_values, obs_precision):
    bands = jnp.repeat(jnp.arange(N_BAND, dtype=jnp.int32), BAND_PATCHES)
    patch_ids = (bands * BAND_PATCHES + patch_order.reshape(-1)).astype(jnp.int32)

    def one(items):
        pid, index, count, values, precision = items
        members = lax.dynamic_index_in_dim(ensemble, pid, 1, keepdims=False)
        return analyse(members, column_operator, index, count, values, precision)
    spreads, results = lax.map(one, (patch_ids, obs_index.reshape(-1, OBS), obs_count.reshape(-1), obs_values.reshape(-1, OBS), obs_precision.reshape(-1, OBS)))
    analysis = jnp.zeros_like(ensemble).at[:, patch_ids, :].set(jnp.swapaxes(results, 0, 1))
    transform = spreads.reshape(N_BAND, BAND_PATCHES, K, K)
    return (analysis, transform)
```

```python
import functools
import math

import jax
import jax.numpy as jnp
from jax import lax
from jax.experimental import pallas as pl
from jax.experimental.pallas import tpu as pltpu
from jax.sharding import PartitionSpec as P

ITERS = 12
LIGHT = 6
CHUNKS = 4
HIGHEST = lax.Precision.HIGHEST


def whole():
    return pl.BlockSpec(memory_space=pltpu.VMEM)


def pieces(x):
    high = x.astype(jnp.bfloat16)
    return high, (x - high.astype(jnp.float32)).astype(jnp.bfloat16)


def product(left, right, full):
    lh, ll = left
    rh, rl = right
    lefts = [lh, lh, ll, ll] if full else [lh, lh, ll]
    rights = [rh, rl, rh, rl] if full else [rh, rl, rh]
    return jnp.dot(
        jnp.concatenate(lefts, axis=1),
        jnp.concatenate(rights, axis=0),
        preferred_element_type=jnp.float32,
    )


def exact(left, right, right_dim=0):
    return lax.dot_general(
        left, right, (((1,), (right_dim,)), ((), ())),
        precision=HIGHEST, preferred_element_type=jnp.float32,
    )


def sweep(y_ref, z_ref, group, full, last):
    for g in range(group):
        y, z = y_ref[g], z_ref[g]
        yp, zp = pieces(y), pieces(z)
        turn = pieces(product(zp, yp, full))
        if not last:
            y_ref[g] = 1.5 * y - 0.5 * product(yp, turn, full)
        z_ref[g] = 1.5 * z - 0.5 * product(turn, zp, full)


def analyse(group, per_worker, first, worker_ref, count_ref, state_ref, op_ref, index_ref, value_ref, weight_ref, *rest):
    spread_ref, out_ref, pert_ref, y_ref, z_ref, row_ref = rest[-6:]
    workers, _, rows_dev, cells = state_ref.shape
    members = workers * rows_dev
    levels = op_ref.shape[0]
    slots = index_ref.shape[1]
    step = pl.program_id(0)
    worker = worker_ref[0]
    eye = (
        lax.broadcasted_iota(jnp.int32, (members, members), 0)
        == lax.broadcasted_iota(jnp.int32, (members, members), 1)
    )
    scales = []
    for g in range(group):
        spot = first + step * group + g
        state = state_ref[:, g].reshape(members, cells)
        mean = jnp.mean(state, axis=0, keepdims=True)
        pert = state - mean
        pert_ref[g] = pert
        op = op_ref[...]
        columns = cells // levels
        chan = jnp.concatenate([exact(pert[:, c * levels:(c + 1) * levels], op) for c in range(columns)], axis=1)
        wide = jnp.broadcast_to(mean, (8, cells))
        chan_mean = jnp.concatenate([exact(wide[:, c * levels:(c + 1) * levels], op) for c in range(columns)], axis=1)
        width = chan.shape[1]
        index = index_ref[pl.ds(worker * per_worker + spot, 1), :]
        live = lax.broadcasted_iota(jnp.int32, (1, slots), 1) < count_ref[spot]
        weight = jnp.where(live, weight_ref[pl.ds(spot, 1), :], 0.0)
        value = weight * value_ref[pl.ds(spot, 1), :]
        picker = (lax.broadcasted_iota(jnp.int32, (width, slots), 0) == index).astype(jnp.bfloat16)
        sub = lax.broadcasted_iota(jnp.int32, (16, slots), 0)
        stack = jnp.where(sub == 0, weight, jnp.where(sub == 1, value, 0.0))
        s0 = stack.astype(jnp.bfloat16)
        left = stack - s0.astype(jnp.float32)
        s1 = left.astype(jnp.bfloat16)
        s2 = (left - s1.astype(jnp.float32)).astype(jnp.bfloat16)
        binned = sum(
            lax.dot_general(s, picker, (((1,), (1,)), ((), ())), preferred_element_type=jnp.float32)
            for s in (s2, s1, s0)
        )
        total = binned[0:1]
        innov = binned[1:2] - chan_mean[0:1] * total
        system = exact(chan * total, chan, 1) + jnp.where(eye, members - 1.0, 0.0)
        row_ref[g] = exact(jnp.broadcast_to(innov, (8, width)), chan, 1)
        trace_value = jnp.sum(jnp.sum(jnp.where(eye, system, 0.0), axis=0, keepdims=True), axis=1, keepdims=True)
        y = system / trace_value
        scales.append(trace_value)
        yp = pieces(y)
        z_ref[g] = jnp.where(eye, 1.5, 0.0) - 0.5 * y
        y_ref[g] = 1.5 * y - 0.5 * product(yp, yp, False)

    def light(k, carry):
        sweep(y_ref, z_ref, group, False, False)
        return carry

    def firm(k, carry):
        sweep(y_ref, z_ref, group, True, False)
        return carry

    lax.fori_loop(1, LIGHT, light, 0)
    lax.fori_loop(LIGHT, ITERS - 1, firm, 0)
    sweep(y_ref, z_ref, group, True, True)

    for g in range(group):
        z = z_ref[g]
        trace_value = scales[g]
        spread = z * (math.sqrt(members - 1.0) / jnp.sqrt(trace_value))
        spread_ref[g] = spread
        weights = exact(exact(row_ref[g], z, 1), z, 1)[0:1] / trace_value
        state_mean = jnp.mean(state_ref[:, g].reshape(members, cells), axis=0, keepdims=True)
        coef = spread + weights
        update = state_mean + product(pieces(coef), pieces(pert_ref[g]), False)
        out_ref[:, g] = update.reshape(workers, rows_dev, cells)


def gather_kernel(n_mem, order_ref, x_ref, *rest):
    outs, lanes_ref = rest[:-1], rest[-1]
    halves, _, lanes = lanes_ref.shape
    for h in range(halves):
        lanes_ref[h] = x_ref[:, h * lanes:(h + 1) * lanes]
    band = order_ref.shape[0]
    per = outs[0].shape[1]
    rows = outs[0].shape[2]
    chunks = len(outs)
    for c, out in enumerate(outs):
        @pl.loop(0, n_mem * per)
        def _(t):
            w, i = t // per, lax.rem(t, per)
            q = order_ref[(w * chunks + c) * per + i]
            for h in range(halves):
                out[w, i, :, h * lanes:(h + 1) * lanes] = lanes_ref[h, pl.ds(q, rows, stride=band), :]


def scatter_kernel(n_mem, order_ref, *refs):
    ins, out, lanes_ref = refs[:-2], refs[-2], refs[-1]
    halves, _, lanes = lanes_ref.shape
    band = order_ref.shape[0]
    per = ins[0].shape[1]
    rows = ins[0].shape[2]
    chunks = len(ins)
    for c, block in enumerate(ins):
        @pl.loop(0, n_mem * per)
        def _(t):
            w, i = t // per, lax.rem(t, per)
            q = order_ref[(w * chunks + c) * per + i]
            for h in range(halves):
                lanes_ref[h, pl.ds(q, rows, stride=band), :] = block[w, i, :, h * lanes:(h + 1) * lanes]

    for h in range(halves):
        out[:, h * lanes:(h + 1) * lanes] = lanes_ref[h]


def local(ensemble, column_operator, patch_order, obs_index, obs_count, obs_values, obs_precision):
    rows_dev, band, cells = ensemble.shape
    slots = obs_index.shape[2]
    n_mem = lax.axis_size("mem")
    per_worker = band // n_mem
    members = rows_dev * n_mem
    chunks = CHUNKS if per_worker % CHUNKS == 0 else 1
    per = per_worker // chunks
    group = 2 if per % 2 == 0 else 1
    order = patch_order[0]
    worker = lax.axis_index("mem").astype(jnp.int32).reshape(1)
    smem = pl.BlockSpec(memory_space=pltpu.SMEM)
    block = jax.ShapeDtypeStruct((n_mem, per, rows_dev, cells), jnp.float32)

    sends = pl.pallas_call(
        functools.partial(gather_kernel, n_mem),
        out_shape=[block] * chunks,
        in_specs=[smem, whole()],
        out_specs=[whole()] * chunks,
        scratch_shapes=[pltpu.VMEM((cells // 128, rows_dev * band, 128), jnp.float32)],
        name="gather_patches",
    )(order, ensemble.reshape(rows_dev * band, cells))

    states = [lax.all_to_all(s, "mem", split_axis=0, concat_axis=0, tiled=True) for s in sends]

    spread_shape = jax.ShapeDtypeStruct((per_worker, members, members), jnp.float32)
    spread = None
    backs = []
    for c in range(chunks):
        first = c * per
        in_specs = [
            pl.BlockSpec((n_mem, group, rows_dev, cells), lambda i, *_: (0, i, 0, 0)),
            whole(), whole(), whole(), whole(),
        ]
        operands = [worker, obs_count[0], states[c], column_operator, obs_index[0], obs_values[0], obs_precision[0]]
        aliases = {}
        if spread is not None:
            in_specs.append(pl.BlockSpec(memory_space=pl.ANY))
            operands.append(spread)
            aliases = {7: 0}
        base = first // group
        spread, updated = pl.pallas_call(
            functools.partial(analyse, group, per_worker, first),
            out_shape=[spread_shape, block],
            grid_spec=pltpu.PrefetchScalarGridSpec(
                num_scalar_prefetch=2,
                grid=(per // group,),
                in_specs=in_specs,
                out_specs=[
                    pl.BlockSpec((group, members, members), lambda i, *_, base=base: (base + i, 0, 0)),
                    pl.BlockSpec((n_mem, group, rows_dev, cells), lambda i, *_: (0, i, 0, 0)),
                ],
                scratch_shapes=[
                    pltpu.VMEM((group, members, cells), jnp.float32),
                    pltpu.VMEM((group, members, members), jnp.float32),
                    pltpu.VMEM((group, members, members), jnp.float32),
                    pltpu.VMEM((group, 8, members), jnp.float32),
                ],
            ),
            input_output_aliases=aliases,
            cost_estimate=pl.CostEstimate(
                flops=per * 36 * 4 * 2 * members ** 3, transcendentals=0,
                bytes_accessed=per * 4 * (2 * members * cells + members * members),
            ),
            name=f"analyse_{c}",
        )(*operands)
        backs.append(lax.all_to_all(updated, "mem", split_axis=0, concat_axis=0, tiled=True))

    restored = pl.pallas_call(
        functools.partial(scatter_kernel, n_mem),
        out_shape=jax.ShapeDtypeStruct((rows_dev * band, cells), jnp.float32),
        in_specs=[smem] + [whole()] * chunks,
        out_specs=whole(),
        scratch_shapes=[pltpu.VMEM((cells // 128, rows_dev * band, 128), jnp.float32)],
        name="restore_patches",
    )(order, *backs)
    return (restored.reshape(rows_dev, band, cells), spread[None])


def solution(mesh):
    placed = (
        P("mem", "band", None),
        P(),
        P("band", None),
        P("band", None, None),
        P("band", "mem"),
        P("band", "mem", None),
        P("band", "mem", None),
    )
    return jax.shard_map(
        local,
        mesh=mesh,
        in_specs=placed,
        out_specs=(P("mem", "band", None), P("band", "mem", None, None)),
        check_vma=False,
    )
```

```python
import functools
import math

import jax
import jax.numpy as jnp
from jax import lax
from jax.experimental import pallas as pl
from jax.experimental.pallas import tpu as pltpu
from jax.sharding import PartitionSpec as P

ITERS = 12
LIGHT = 6
MESH = pl.DeviceIdType.MESH
HIGHEST = lax.Precision.HIGHEST


def whole():
    return pl.BlockSpec(memory_space=pltpu.VMEM)


def pieces(x):
    high = x.astype(jnp.bfloat16)
    return high, (x - high.astype(jnp.float32)).astype(jnp.bfloat16)


def product(left, right, full):
    lh, ll = left
    rh, rl = right
    lefts = [lh, lh, ll, ll] if full else [lh, lh, ll]
    rights = [rh, rl, rh, rl] if full else [rh, rl, rh]
    return jnp.dot(
        jnp.concatenate(lefts, axis=1),
        jnp.concatenate(rights, axis=0),
        preferred_element_type=jnp.float32,
    )


def exact(left, right, right_dim=0):
    return lax.dot_general(
        left, right, (((1,), (right_dim,)), ((), ())),
        precision=HIGHEST, preferred_element_type=jnp.float32,
    )


def sweep(y_ref, z_ref, group, full, last):
    for g in range(group):
        y, z = y_ref[g], z_ref[g]
        yp, zp = pieces(y), pieces(z)
        turn = pieces(product(zp, yp, full))
        if not last:
            y_ref[g] = 1.5 * y - 0.5 * product(yp, turn, full)
        z_ref[g] = 1.5 * z - 0.5 * product(turn, zp, full)


def analyse(n_mem, group, count_ref, sends_ref, op_ref, index_ref, value_ref, weight_ref, spread_ref, back_ref,
            inbox, outbox, pert_ref, y_ref, z_ref, row_ref, in_send, in_recv, own_sem, out_send, out_recv, home_sem):
    per_worker, workers, rows_dev, cells = inbox.shape
    members = workers * rows_dev
    levels = op_ref.shape[0]
    slots = index_ref.shape[1]
    me = lax.axis_index("mem")

    def greet(d, carry):
        pl.semaphore_signal(barrier, inc=1, device_id={"mem": lax.rem(me + d, n_mem)}, device_id_type=MESH)
        return carry

    barrier = pltpu.get_barrier_semaphore()
    lax.fori_loop(1, n_mem, greet, 0)
    pl.semaphore_wait(barrier, n_mem - 1)

    def own_in(i):
        return pltpu.make_async_copy(sends_ref.at[me, i], inbox.at[i, me], own_sem.at[i])

    def own_back(i):
        return pltpu.make_async_copy(outbox.at[i, me], back_ref.at[me, i], home_sem.at[i])

    def issue(i, carry):
        own_in(i).start()

        def one(d, carry):
            peer = lax.rem(me + d, n_mem)
            pltpu.make_async_remote_copy(
                src_ref=sends_ref.at[peer, i], dst_ref=inbox.at[i, me],
                send_sem=in_send, recv_sem=in_recv.at[i],
                device_id={"mem": peer}, device_id_type=MESH,
            ).start()
            return carry

        lax.fori_loop(1, n_mem, one, 0)
        return carry

    lax.fori_loop(0, per_worker, issue, 0)
    eye = (
        lax.broadcasted_iota(jnp.int32, (members, members), 0)
        == lax.broadcasted_iota(jnp.int32, (members, members), 1)
    )

    def step(t, carry):
        for g in range(group):
            spot = t * group + g
            own_in(spot).wait()
            arrived = inbox.at[spot, pl.ds(0, n_mem - 1)]
            pltpu.make_async_copy(arrived, arrived, in_recv.at[spot]).wait()
        scales = []
        for g in range(group):
            scales.append(prepare(t * group + g, g))
        lax.fori_loop(1, LIGHT, light, 0)
        lax.fori_loop(LIGHT, ITERS - 1, firm, 0)
        sweep(y_ref, z_ref, group, True, True)
        for g in range(group):
            finish(t * group + g, g, scales[g])
            launch(t * group + g)
        return carry

    def launch(spot):
        own_back(spot).start()

        def one(d, carry):
            peer = lax.rem(me + d, n_mem)
            pltpu.make_async_remote_copy(
                src_ref=outbox.at[spot, peer], dst_ref=back_ref.at[me, spot],
                send_sem=out_send, recv_sem=out_recv,
                device_id={"mem": peer}, device_id_type=MESH,
            ).start()
            return carry

        lax.fori_loop(1, n_mem, one, 0)

    def prepare(spot, g):
        state = inbox[spot].reshape(members, cells)
        mean = jnp.mean(state, axis=0, keepdims=True)
        pert = state - mean
        pert_ref[g] = pert
        op = op_ref[...]
        columns = cells // levels
        chan = jnp.concatenate([exact(pert[:, c * levels:(c + 1) * levels], op) for c in range(columns)], axis=1)
        wide = jnp.broadcast_to(mean, (8, cells))
        chan_mean = jnp.concatenate([exact(wide[:, c * levels:(c + 1) * levels], op) for c in range(columns)], axis=1)
        width = chan.shape[1]
        index = index_ref[pl.ds(me * per_worker + spot, 1), :]
        live = lax.broadcasted_iota(jnp.int32, (1, slots), 1) < count_ref[spot]
        weight = jnp.where(live, weight_ref[pl.ds(spot, 1), :], 0.0)
        value = weight * value_ref[pl.ds(spot, 1), :]
        picker = (lax.broadcasted_iota(jnp.int32, (width, slots), 0) == index).astype(jnp.bfloat16)
        sub = lax.broadcasted_iota(jnp.int32, (16, slots), 0)
        stack = jnp.where(sub == 0, weight, jnp.where(sub == 1, value, 0.0))
        s0 = stack.astype(jnp.bfloat16)
        left = stack - s0.astype(jnp.float32)
        s1 = left.astype(jnp.bfloat16)
        s2 = (left - s1.astype(jnp.float32)).astype(jnp.bfloat16)
        binned = sum(
            lax.dot_general(s, picker, (((1,), (1,)), ((), ())), preferred_element_type=jnp.float32)
            for s in (s2, s1, s0)
        )
        total = binned[0:1]
        innov = binned[1:2] - chan_mean[0:1] * total
        system = exact(chan * total, chan, 1) + jnp.where(eye, members - 1.0, 0.0)
        row_ref[g] = exact(jnp.broadcast_to(innov, (8, width)), chan, 1)
        trace_value = jnp.sum(jnp.sum(jnp.where(eye, system, 0.0), axis=0, keepdims=True), axis=1, keepdims=True)
        y = system / trace_value
        yp = pieces(y)
        z_ref[g] = jnp.where(eye, 1.5, 0.0) - 0.5 * y
        y_ref[g] = 1.5 * y - 0.5 * product(yp, yp, False)
        return trace_value

    def light(k, carry):
        sweep(y_ref, z_ref, group, False, False)
        return carry

    def firm(k, carry):
        sweep(y_ref, z_ref, group, True, False)
        return carry

    def finish(spot, g, trace_value):
        z = z_ref[g]
        spread = z * (math.sqrt(members - 1.0) / jnp.sqrt(trace_value))
        spread_ref[spot] = spread
        weights = exact(exact(row_ref[g], z, 1), z, 1)[0:1] / trace_value
        state_mean = jnp.mean(inbox[spot].reshape(members, cells), axis=0, keepdims=True)
        coef = spread + weights
        update = state_mean + product(pieces(coef), pieces(pert_ref[g]), False)
        outbox[spot] = update.reshape(workers, rows_dev, cells)

    lax.fori_loop(0, per_worker // group, step, 0)
    sent = sends_ref.at[pl.ds(0, n_mem - 1)]
    pltpu.make_async_copy(sent, sent, in_send).wait()
    posted = back_ref.at[pl.ds(0, n_mem - 1)]
    pltpu.make_async_copy(posted, posted, out_send).wait()
    pltpu.make_async_copy(posted, posted, out_recv).wait()
    for i in range(per_worker):
        own_back(i).wait()


def gather_kernel(n_mem, order_ref, x_ref, *rest):
    outs, lanes_ref = rest[:-1], rest[-1]
    halves, _, lanes = lanes_ref.shape
    for h in range(halves):
        lanes_ref[h] = x_ref[:, h * lanes:(h + 1) * lanes]
    band = order_ref.shape[0]
    per = outs[0].shape[1]
    rows = outs[0].shape[2]
    chunks = len(outs)
    for c, out in enumerate(outs):
        @pl.loop(0, n_mem * per)
        def _(t):
            w, i = t // per, lax.rem(t, per)
            q = order_ref[(w * chunks + c) * per + i]
            for h in range(halves):
                out[w, i, :, h * lanes:(h + 1) * lanes] = lanes_ref[h, pl.ds(q, rows, stride=band), :]


def scatter_kernel(n_mem, order_ref, *refs):
    ins, out, lanes_ref = refs[:-2], refs[-2], refs[-1]
    halves, _, lanes = lanes_ref.shape
    band = order_ref.shape[0]
    per = ins[0].shape[1]
    rows = ins[0].shape[2]
    chunks = len(ins)
    for c, block in enumerate(ins):
        @pl.loop(0, n_mem * per)
        def _(t):
            w, i = t // per, lax.rem(t, per)
            q = order_ref[(w * chunks + c) * per + i]
            for h in range(halves):
                lanes_ref[h, pl.ds(q, rows, stride=band), :] = block[w, i, :, h * lanes:(h + 1) * lanes]

    for h in range(halves):
        out[:, h * lanes:(h + 1) * lanes] = lanes_ref[h]


def local(ensemble, column_operator, patch_order, obs_index, obs_count, obs_values, obs_precision):
    rows_dev, band, cells = ensemble.shape
    slots = obs_index.shape[2]
    n_mem = lax.axis_size("mem")
    per_worker = band // n_mem
    members = rows_dev * n_mem
    group = 2 if per_worker % 2 == 0 else 1
    order = patch_order[0]
    smem = pl.BlockSpec(memory_space=pltpu.SMEM)
    block = jax.ShapeDtypeStruct((n_mem, per_worker, rows_dev, cells), jnp.float32)

    sends, = pl.pallas_call(
        functools.partial(gather_kernel, n_mem),
        out_shape=[block],
        in_specs=[smem, whole()],
        out_specs=[whole()],
        scratch_shapes=[pltpu.VMEM((cells // 128, rows_dev * band, 128), jnp.float32)],
        name="gather_patches",
    )(order, ensemble.reshape(rows_dev * band, cells))

    spread, back = pl.pallas_call(
        functools.partial(analyse, n_mem, group),
        out_shape=[jax.ShapeDtypeStruct((per_worker, members, members), jnp.float32), block],
        in_specs=[smem, pl.BlockSpec(memory_space=pl.ANY), whole(), whole(), whole(), whole()],
        out_specs=[whole(), pl.BlockSpec(memory_space=pl.ANY)],
        scratch_shapes=[
            pltpu.VMEM((per_worker, n_mem, rows_dev, cells), jnp.float32),
            pltpu.VMEM((per_worker, n_mem, rows_dev, cells), jnp.float32),
            pltpu.VMEM((group, members, cells), jnp.float32),
            pltpu.VMEM((group, members, members), jnp.float32),
            pltpu.VMEM((group, members, members), jnp.float32),
            pltpu.VMEM((group, 8, members), jnp.float32),
            pltpu.SemaphoreType.DMA(()),
            pltpu.SemaphoreType.DMA((per_worker,)),
            pltpu.SemaphoreType.DMA((per_worker,)),
            pltpu.SemaphoreType.DMA(()),
            pltpu.SemaphoreType.DMA(()),
            pltpu.SemaphoreType.DMA((per_worker,)),
        ],
        compiler_params=pltpu.CompilerParams(collective_id=0, has_side_effects=True),
        name="analyse",
    )(obs_count[0], sends, column_operator, obs_index[0], obs_values[0], obs_precision[0])

    restored = pl.pallas_call(
        functools.partial(scatter_kernel, n_mem),
        out_shape=jax.ShapeDtypeStruct((rows_dev * band, cells), jnp.float32),
        in_specs=[smem] + [whole()],
        out_specs=whole(),
        scratch_shapes=[pltpu.VMEM((cells // 128, rows_dev * band, 128), jnp.float32)],
        name="restore_patches",
    )(order, back)
    return (restored.reshape(rows_dev, band, cells), spread[None])


def solution(mesh):
    placed = (
        P("mem", "band", None),
        P(),
        P("band", None),
        P("band", None, None),
        P("band", "mem"),
        P("band", "mem", None),
        P("band", "mem", None),
    )
    return jax.shard_map(
        local,
        mesh=mesh,
        in_specs=placed,
        out_specs=(P("mem", "band", None), P("band", "mem", None, None)),
        check_vma=False,
    )
```

```python
import functools
import math

import jax
import jax.numpy as jnp
from jax import lax
from jax.experimental import pallas as pl
from jax.experimental.pallas import tpu as pltpu
from jax.sharding import PartitionSpec as P

ITERS = 12
LIGHT = 8
MESH = pl.DeviceIdType.MESH
HIGHEST = lax.Precision.HIGHEST


def whole():
    return pl.BlockSpec(memory_space=pltpu.VMEM)


def pieces(x):
    high = x.astype(jnp.bfloat16)
    return high, (x - high.astype(jnp.float32)).astype(jnp.bfloat16)


def product(left, right, full, right_dim=0):
    lh, ll = left
    rh, rl = right
    lefts = [lh, lh, ll, ll] if full else [lh, lh, ll]
    rights = [rh, rl, rh, rl] if full else [rh, rl, rh]
    return lax.dot_general(
        jnp.concatenate(lefts, axis=1),
        jnp.concatenate(rights, axis=right_dim),
        (((1,), (right_dim,)), ((), ())),
        preferred_element_type=jnp.float32,
    )


def exact(left, right, right_dim=0):
    return lax.dot_general(
        left, right, (((1,), (right_dim,)), ((), ())),
        precision=HIGHEST, preferred_element_type=jnp.float32,
    )


def sweep(y_ref, z_ref, group, full, last):
    for g in range(group):
        y, z = y_ref[g], z_ref[g]
        yp, zp = pieces(y), pieces(z)
        turn = pieces(product(zp, yp, full))
        if not last:
            y_ref[g] = 1.5 * y - 0.5 * product(yp, turn, full)
        z_ref[g] = 1.5 * z - 0.5 * product(turn, zp, full)


def analyse(n_mem, group, order_ref, count_ref, x_ref, op_ref, index_ref, value_ref, weight_ref, spread_ref, back_ref,
            lanes_ref, sends_ref, inbox, outbox, pert_ref, y_ref, z_ref, col_ref, mean_ref, in_send, in_recv, own_sem, out_send, out_recv, home_sem):
    per_worker, workers, rows_dev, cells = inbox.shape
    members = workers * rows_dev
    levels = op_ref.shape[0]
    slots = index_ref.shape[1]
    me = lax.axis_index("mem")

    def greet(d, carry):
        pl.semaphore_signal(barrier, inc=1, device_id={"mem": lax.rem(me + d, n_mem)}, device_id_type=MESH)
        return carry

    barrier = pltpu.get_barrier_semaphore()
    lax.fori_loop(1, n_mem, greet, 0)
    halves, _, lanes = lanes_ref.shape
    band = order_ref.shape[0]
    for h in range(halves):
        lanes_ref[h] = x_ref[:, h * lanes:(h + 1) * lanes]

    def stage(i):
        def one(w, carry):
            q = order_ref[w * per_worker + i]
            for h in range(halves):
                sends_ref[w, i, :, h * lanes:(h + 1) * lanes] = lanes_ref[h, pl.ds(q, rows_dev, stride=band), :]
            return carry

        lax.fori_loop(0, n_mem, one, 0)

    stage(0)
    pl.semaphore_wait(barrier, n_mem - 1)

    def own_in(i):
        return pltpu.make_async_copy(sends_ref.at[me, i], inbox.at[i, me], own_sem.at[i])

    def own_back(i):
        return pltpu.make_async_copy(outbox.at[i, me], back_ref.at[me, i], home_sem.at[i])

    def issue(i):
        own_in(i).start()

        def one(d, carry):
            peer = lax.rem(me + d, n_mem)
            pltpu.make_async_remote_copy(
                src_ref=sends_ref.at[peer, i], dst_ref=inbox.at[i, me],
                send_sem=in_send, recv_sem=in_recv.at[i],
                device_id={"mem": peer}, device_id_type=MESH,
            ).start()
            return carry

        lax.fori_loop(1, n_mem, one, 0)

    def feed(i, carry):
        stage(i + 1)
        issue(i)
        return carry

    lax.fori_loop(0, per_worker - 1, feed, 0)
    issue(per_worker - 1)
    eye = (
        lax.broadcasted_iota(jnp.int32, (members, members), 0)
        == lax.broadcasted_iota(jnp.int32, (members, members), 1)
    )

    def step(t, carry):
        for g in range(group):
            spot = t * group + g
            own_in(spot).wait()
            arrived = inbox.at[spot, pl.ds(0, n_mem - 1)]
            pltpu.make_async_copy(arrived, arrived, in_recv.at[spot]).wait()
        scales = []
        for g in range(group):
            scales.append(prepare(t * group + g, g))
        lax.fori_loop(1, LIGHT, light, 0)
        lax.fori_loop(LIGHT, ITERS - 1, firm, 0)
        sweep(y_ref, z_ref, group, True, True)
        for g in range(group):
            finish(t * group + g, g, scales[g])
            launch(t * group + g)
        return carry

    def launch(spot):
        own_back(spot).start()

        def one(d, carry):
            peer = lax.rem(me + d, n_mem)
            pltpu.make_async_remote_copy(
                src_ref=outbox.at[spot, peer], dst_ref=back_ref.at[me, spot],
                send_sem=out_send, recv_sem=out_recv,
                device_id={"mem": peer}, device_id_type=MESH,
            ).start()
            return carry

        lax.fori_loop(1, n_mem, one, 0)

    def prepare(spot, g):
        state = inbox[spot].reshape(members, cells)
        mean = jnp.mean(state, axis=0, keepdims=True)
        pert = state - mean
        pert_ref[g] = pert
        op = op_ref[...]
        columns = cells // levels
        op_pieces = pieces(op)
        chan = jnp.concatenate([product(pieces(pert[:, c * levels:(c + 1) * levels]), op_pieces, False) for c in range(columns)], axis=1)
        wide = jnp.broadcast_to(mean, (8, cells))
        chan_mean = jnp.concatenate([exact(wide[:, c * levels:(c + 1) * levels], op) for c in range(columns)], axis=1)
        width = chan.shape[1]
        index = index_ref[pl.ds(me * per_worker + spot, 1), :]
        live = lax.broadcasted_iota(jnp.int32, (1, slots), 1) < count_ref[spot]
        weight = jnp.where(live, weight_ref[pl.ds(spot, 1), :], 0.0)
        value = weight * value_ref[pl.ds(spot, 1), :]
        picker = (lax.broadcasted_iota(jnp.int32, (width, slots), 0) == index).astype(jnp.bfloat16)
        sub = lax.broadcasted_iota(jnp.int32, (16, slots), 0)
        stack = jnp.where(sub == 0, weight, jnp.where(sub == 1, value, 0.0))
        s0 = stack.astype(jnp.bfloat16)
        left = stack - s0.astype(jnp.float32)
        s1 = left.astype(jnp.bfloat16)
        s2 = (left - s1.astype(jnp.float32)).astype(jnp.bfloat16)
        binned = lax.dot_general(
            jnp.concatenate([s0, s1, s2], axis=0), picker, (((1,), (1,)), ((), ())),
            preferred_element_type=jnp.float32,
        )
        binned = binned[0:16] + (binned[16:32] + binned[32:48])
        total = binned[0:1]
        innov = binned[1:2] - chan_mean[0:1] * total
        system = exact(chan * total, chan, 1) + jnp.where(eye, members - 1.0, 0.0)
        col_ref[g] = jnp.sum(chan * innov, axis=1, keepdims=True)
        mean_ref[g] = wide
        trace_value = jnp.sum(jnp.sum(jnp.where(eye, system, 0.0), axis=0, keepdims=True), axis=1, keepdims=True)
        y = system / trace_value
        yp = pieces(y)
        z_ref[g] = jnp.where(eye, 1.5, 0.0) - 0.5 * y
        y_ref[g] = 1.5 * y - 0.5 * product(yp, yp, False)
        return trace_value

    def light(k, carry):
        sweep(y_ref, z_ref, group, False, False)
        return carry

    def firm(k, carry):
        sweep(y_ref, z_ref, group, True, False)
        return carry

    def finish(spot, g, trace_value):
        z = z_ref[g]
        spread = z * (math.sqrt(members - 1.0) / jnp.sqrt(trace_value))
        spread_ref[spot] = spread
        inner = jnp.sum(z * col_ref[g], axis=0, keepdims=True)
        weights = jnp.sum(z * inner, axis=1, keepdims=True) / trace_value
        pert = pert_ref[g]
        shift = mean_ref[g][0:1] + jnp.sum(pert * weights, axis=0, keepdims=True)
        update = shift + product(pieces(spread), pieces(pert), False)
        outbox[spot] = update.reshape(workers, rows_dev, cells)

    lax.fori_loop(0, per_worker // group, step, 0)
    sent = sends_ref.at[pl.ds(0, n_mem - 1)]
    pltpu.make_async_copy(sent, sent, in_send).wait()
    posted = back_ref.at[pl.ds(0, n_mem - 1)]
    pltpu.make_async_copy(posted, posted, out_send).wait()
    pltpu.make_async_copy(posted, posted, out_recv).wait()
    for i in range(per_worker):
        own_back(i).wait()


def scatter_kernel(n_mem, order_ref, *refs):
    ins, out, lanes_ref = refs[:-2], refs[-2], refs[-1]
    halves, _, lanes = lanes_ref.shape
    band = order_ref.shape[0]
    per = ins[0].shape[1]
    rows = ins[0].shape[2]
    chunks = len(ins)
    for c, block in enumerate(ins):
        @pl.loop(0, n_mem * per)
        def _(t):
            w, i = t // per, lax.rem(t, per)
            q = order_ref[(w * chunks + c) * per + i]
            for h in range(halves):
                lanes_ref[h, pl.ds(q, rows, stride=band), :] = block[w, i, :, h * lanes:(h + 1) * lanes]

    for h in range(halves):
        out[:, h * lanes:(h + 1) * lanes] = lanes_ref[h]


def local(ensemble, column_operator, patch_order, obs_index, obs_count, obs_values, obs_precision):
    rows_dev, band, cells = ensemble.shape
    slots = obs_index.shape[2]
    n_mem = lax.axis_size("mem")
    per_worker = band // n_mem
    members = rows_dev * n_mem
    group = 2 if per_worker % 2 == 0 else 1
    order = patch_order[0]
    smem = pl.BlockSpec(memory_space=pltpu.SMEM)
    block = jax.ShapeDtypeStruct((n_mem, per_worker, rows_dev, cells), jnp.float32)

    spread, back = pl.pallas_call(
        functools.partial(analyse, n_mem, group),
        out_shape=[jax.ShapeDtypeStruct((per_worker, members, members), jnp.float32), block],
        in_specs=[smem, smem, whole(), whole(), whole(), whole(), whole()],
        out_specs=[whole(), pl.BlockSpec(memory_space=pl.ANY)],
        scratch_shapes=[
            pltpu.VMEM((cells // 128, rows_dev * band, 128), jnp.float32),
            pltpu.VMEM((n_mem, per_worker, rows_dev, cells), jnp.float32),
            pltpu.VMEM((per_worker, n_mem, rows_dev, cells), jnp.float32),
            pltpu.VMEM((per_worker, n_mem, rows_dev, cells), jnp.float32),
            pltpu.VMEM((group, members, cells), jnp.float32),
            pltpu.VMEM((group, members, members), jnp.float32),
            pltpu.VMEM((group, members, members), jnp.float32),
            pltpu.VMEM((group, members, 1), jnp.float32),
            pltpu.VMEM((group, 8, cells), jnp.float32),
            pltpu.SemaphoreType.DMA(()),
            pltpu.SemaphoreType.DMA((per_worker,)),
            pltpu.SemaphoreType.DMA((per_worker,)),
            pltpu.SemaphoreType.DMA(()),
            pltpu.SemaphoreType.DMA(()),
            pltpu.SemaphoreType.DMA((per_worker,)),
        ],
        compiler_params=pltpu.CompilerParams(collective_id=0, has_side_effects=True),
        name="analyse",
    )(order, obs_count[0], ensemble.reshape(rows_dev * band, cells), column_operator, obs_index[0], obs_values[0], obs_precision[0])

    restored = pl.pallas_call(
        functools.partial(scatter_kernel, n_mem),
        out_shape=jax.ShapeDtypeStruct((rows_dev * band, cells), jnp.float32),
        in_specs=[smem] + [whole()],
        out_specs=whole(),
        scratch_shapes=[pltpu.VMEM((cells // 128, rows_dev * band, 128), jnp.float32)],
        name="restore_patches",
    )(order, back)
    return (restored.reshape(rows_dev, band, cells), spread[None])


def solution(mesh):
    placed = (
        P("mem", "band", None),
        P(),
        P("band", None),
        P("band", None, None),
        P("band", "mem"),
        P("band", "mem", None),
        P("band", "mem", None),
    )
    return jax.shard_map(
        local,
        mesh=mesh,
        in_specs=placed,
        out_specs=(P("mem", "band", None), P("band", "mem", None, None)),
        check_vma=False,
    )
```

```python
import functools
import math

import jax
import jax.numpy as jnp
from jax import lax
from jax.experimental import pallas as pl
from jax.experimental.pallas import tpu as pltpu
from jax.sharding import PartitionSpec as P

ITERS = 12
LIGHT = 8
MESH = pl.DeviceIdType.MESH
HIGHEST = lax.Precision.HIGHEST


def whole():
    return pl.BlockSpec(memory_space=pltpu.VMEM)


def pieces(x):
    high = x.astype(jnp.bfloat16)
    return high, (x - high.astype(jnp.float32)).astype(jnp.bfloat16)


def product(left, right, full, right_dim=0):
    lh, ll = left
    rh, rl = right
    lefts = [lh, lh, ll, ll] if full else [lh, lh, ll]
    rights = [rh, rl, rh, rl] if full else [rh, rl, rh]
    return lax.dot_general(
        jnp.concatenate(lefts, axis=1),
        jnp.concatenate(rights, axis=right_dim),
        (((1,), (right_dim,)), ((), ())),
        preferred_element_type=jnp.float32,
    )


def exact(left, right, right_dim=0):
    return lax.dot_general(
        left, right, (((1,), (right_dim,)), ((), ())),
        precision=HIGHEST, preferred_element_type=jnp.float32,
    )


def sweep(y_ref, z_ref, group, full, last):
    for g in range(group):
        y, z = y_ref[g], z_ref[g]
        yp, zp = pieces(y), pieces(z)
        turn = pieces(product(zp, yp, full))
        if not last:
            y_ref[g] = 1.5 * y - 0.5 * product(yp, turn, full)
        z_ref[g] = 1.5 * z - 0.5 * product(turn, zp, full)


def analyse(n_mem, group, order_ref, count_ref, x_ref, op_ref, index_ref, value_ref, weight_ref, spread_ref, back_ref,
            lanes_ref, sends_ref, inbox, outbox, pert_ref, y_ref, z_ref, col_ref, mean_ref, in_send, in_recv, own_sem, out_send, out_recv, home_sem):
    per_worker, workers, rows_dev, cells = inbox.shape
    members = workers * rows_dev
    levels = op_ref.shape[0]
    slots = index_ref.shape[1]
    me = lax.axis_index("mem")

    def greet(d, carry):
        pl.semaphore_signal(barrier, inc=1, device_id={"mem": lax.rem(me + d, n_mem)}, device_id_type=MESH)
        return carry

    barrier = pltpu.get_barrier_semaphore()
    lax.fori_loop(1, n_mem, greet, 0)
    halves, _, lanes = lanes_ref.shape
    band = order_ref.shape[0]
    for h in range(halves):
        lanes_ref[h] = x_ref[:, h * lanes:(h + 1) * lanes]

    def stage(i):
        def one(w, carry):
            q = order_ref[w * per_worker + i]
            for h in range(halves):
                sends_ref[w, i, :, h * lanes:(h + 1) * lanes] = lanes_ref[h, pl.ds(q, rows_dev, stride=band), :]
            return carry

        lax.fori_loop(0, n_mem, one, 0)

    stage(0)
    pl.semaphore_wait(barrier, n_mem - 1)

    def own_in(i):
        return pltpu.make_async_copy(sends_ref.at[me, i], inbox.at[i, me], own_sem.at[i])

    def own_back(i):
        return pltpu.make_async_copy(outbox.at[i, me], back_ref.at[me, i], home_sem.at[i])

    def issue(i):
        own_in(i).start()

        def one(d, carry):
            peer = lax.rem(me + d, n_mem)
            pltpu.make_async_remote_copy(
                src_ref=sends_ref.at[peer, i], dst_ref=inbox.at[i, me],
                send_sem=in_send, recv_sem=in_recv.at[i],
                device_id={"mem": peer}, device_id_type=MESH,
            ).start()
            return carry

        lax.fori_loop(1, n_mem, one, 0)

    def feed(i, carry):
        stage(i + 1)
        issue(i)
        return carry

    lax.fori_loop(0, per_worker - 1, feed, 0)
    issue(per_worker - 1)
    eye = (
        lax.broadcasted_iota(jnp.int32, (members, members), 0)
        == lax.broadcasted_iota(jnp.int32, (members, members), 1)
    )

    def run(base, size):
        for g in range(size):
            own_in(base + g).wait()
            arrived = inbox.at[base + g, pl.ds(0, n_mem - 1)]
            pltpu.make_async_copy(arrived, arrived, in_recv.at[base + g]).wait()
        scales = [prepare(base + g, g) for g in range(size)]

        def light(k, carry):
            sweep(y_ref, z_ref, size, False, False)
            return carry

        def firm(k, carry):
            sweep(y_ref, z_ref, size, True, False)
            return carry

        lax.fori_loop(1, LIGHT, light, 0)
        lax.fori_loop(LIGHT, ITERS - 1, firm, 0)
        sweep(y_ref, z_ref, size, True, True)
        for g in range(size):
            finish(base + g, g, scales[g])
            launch(base + g)

    def launch(spot):
        own_back(spot).start()

        def one(d, carry):
            peer = lax.rem(me + d, n_mem)
            pltpu.make_async_remote_copy(
                src_ref=outbox.at[spot, peer], dst_ref=back_ref.at[me, spot],
                send_sem=out_send, recv_sem=out_recv,
                device_id={"mem": peer}, device_id_type=MESH,
            ).start()
            return carry

        lax.fori_loop(1, n_mem, one, 0)

    def prepare(spot, g):
        state = inbox[spot].reshape(members, cells)
        mean = jnp.mean(state, axis=0, keepdims=True)
        pert = state - mean
        pert_ref[g] = pert
        op = op_ref[...]
        columns = cells // levels
        op_pieces = pieces(op)
        chan = jnp.concatenate([product(pieces(pert[:, c * levels:(c + 1) * levels]), op_pieces, False) for c in range(columns)], axis=1)
        wide = jnp.broadcast_to(mean, (8, cells))
        chan_mean = jnp.concatenate([exact(wide[:, c * levels:(c + 1) * levels], op) for c in range(columns)], axis=1)
        width = chan.shape[1]
        index = index_ref[pl.ds(me * per_worker + spot, 1), :]
        live = lax.broadcasted_iota(jnp.int32, (1, slots), 1) < count_ref[spot]
        weight = jnp.where(live, weight_ref[pl.ds(spot, 1), :], 0.0)
        value = weight * value_ref[pl.ds(spot, 1), :]
        picker = (lax.broadcasted_iota(jnp.int32, (width, slots), 0) == index).astype(jnp.bfloat16)
        sub = lax.broadcasted_iota(jnp.int32, (16, slots), 0)
        stack = jnp.where(sub == 0, weight, jnp.where(sub == 1, value, 0.0))
        s0 = stack.astype(jnp.bfloat16)
        left = stack - s0.astype(jnp.float32)
        s1 = left.astype(jnp.bfloat16)
        s2 = (left - s1.astype(jnp.float32)).astype(jnp.bfloat16)
        binned = lax.dot_general(
            jnp.concatenate([s0, s1, s2], axis=0), picker, (((1,), (1,)), ((), ())),
            preferred_element_type=jnp.float32,
        )
        binned = binned[0:16] + (binned[16:32] + binned[32:48])
        total = binned[0:1]
        innov = binned[1:2] - chan_mean[0:1] * total
        system = exact(chan * total, chan, 1) + jnp.where(eye, members - 1.0, 0.0)
        col_ref[g] = jnp.sum(chan * innov, axis=1, keepdims=True)
        mean_ref[g] = wide
        trace_value = jnp.sum(jnp.sum(jnp.where(eye, system, 0.0), axis=0, keepdims=True), axis=1, keepdims=True)
        y = system / trace_value
        yp = pieces(y)
        z_ref[g] = jnp.where(eye, 1.5, 0.0) - 0.5 * y
        y_ref[g] = 1.5 * y - 0.5 * product(yp, yp, False)
        return trace_value

    def finish(spot, g, trace_value):
        z = z_ref[g]
        spread = z * (math.sqrt(members - 1.0) / jnp.sqrt(trace_value))
        spread_ref[spot] = spread
        inner = jnp.sum(z * col_ref[g], axis=0, keepdims=True)
        weights = jnp.sum(z * inner, axis=1, keepdims=True) / trace_value
        pert = pert_ref[g]
        shift = mean_ref[g][0:1] + jnp.sum(pert * weights, axis=0, keepdims=True)
        update = shift + product(pieces(spread), pieces(pert), False)
        outbox[spot] = update.reshape(workers, rows_dev, cells)

    edge = 1 if group > 1 and per_worker % group == 0 and per_worker > group else 0
    middle = (per_worker - 2 * edge) // group

    def step(t, carry):
        run(edge + t * group, group)
        return carry

    if edge:
        run(0, 1)
    lax.fori_loop(0, middle, step, 0)
    if edge:
        run(per_worker - 1, 1)
    sent = sends_ref.at[pl.ds(0, n_mem - 1)]
    pltpu.make_async_copy(sent, sent, in_send).wait()
    posted = back_ref.at[pl.ds(0, n_mem - 1)]
    pltpu.make_async_copy(posted, posted, out_send).wait()
    pltpu.make_async_copy(posted, posted, out_recv).wait()
    for i in range(per_worker):
        own_back(i).wait()


def scatter_kernel(n_mem, order_ref, *refs):
    ins, out, lanes_ref = refs[:-2], refs[-2], refs[-1]
    halves, _, lanes = lanes_ref.shape
    band = order_ref.shape[0]
    per = ins[0].shape[1]
    rows = ins[0].shape[2]
    chunks = len(ins)
    for c, block in enumerate(ins):
        @pl.loop(0, n_mem * per)
        def _(t):
            w, i = t // per, lax.rem(t, per)
            q = order_ref[(w * chunks + c) * per + i]
            for h in range(halves):
                lanes_ref[h, pl.ds(q, rows, stride=band), :] = block[w, i, :, h * lanes:(h + 1) * lanes]

    for h in range(halves):
        out[:, h * lanes:(h + 1) * lanes] = lanes_ref[h]


def local(ensemble, column_operator, patch_order, obs_index, obs_count, obs_values, obs_precision):
    rows_dev, band, cells = ensemble.shape
    slots = obs_index.shape[2]
    n_mem = lax.axis_size("mem")
    per_worker = band // n_mem
    members = rows_dev * n_mem
    group = 2 if per_worker % 2 == 0 else 1
    order = patch_order[0]
    smem = pl.BlockSpec(memory_space=pltpu.SMEM)
    block = jax.ShapeDtypeStruct((n_mem, per_worker, rows_dev, cells), jnp.float32)

    spread, back = pl.pallas_call(
        functools.partial(analyse, n_mem, group),
        out_shape=[jax.ShapeDtypeStruct((per_worker, members, members), jnp.float32), block],
        in_specs=[smem, smem, whole(), whole(), whole(), whole(), whole()],
        out_specs=[whole(), pl.BlockSpec(memory_space=pl.ANY)],
        scratch_shapes=[
            pltpu.VMEM((cells // 128, rows_dev * band, 128), jnp.float32),
            pltpu.VMEM((n_mem, per_worker, rows_dev, cells), jnp.float32),
            pltpu.VMEM((per_worker, n_mem, rows_dev, cells), jnp.float32),
            pltpu.VMEM((per_worker, n_mem, rows_dev, cells), jnp.float32),
            pltpu.VMEM((group, members, cells), jnp.float32),
            pltpu.VMEM((group, members, members), jnp.float32),
            pltpu.VMEM((group, members, members), jnp.float32),
            pltpu.VMEM((group, members, 1), jnp.float32),
            pltpu.VMEM((group, 8, cells), jnp.float32),
            pltpu.SemaphoreType.DMA(()),
            pltpu.SemaphoreType.DMA((per_worker,)),
            pltpu.SemaphoreType.DMA((per_worker,)),
            pltpu.SemaphoreType.DMA(()),
            pltpu.SemaphoreType.DMA(()),
            pltpu.SemaphoreType.DMA((per_worker,)),
        ],
        compiler_params=pltpu.CompilerParams(collective_id=0, has_side_effects=True),
        name="analyse",
    )(order, obs_count[0], ensemble.reshape(rows_dev * band, cells), column_operator, obs_index[0], obs_values[0], obs_precision[0])

    restored = pl.pallas_call(
        functools.partial(scatter_kernel, n_mem),
        out_shape=jax.ShapeDtypeStruct((rows_dev * band, cells), jnp.float32),
        in_specs=[smem] + [whole()],
        out_specs=whole(),
        scratch_shapes=[pltpu.VMEM((cells // 128, rows_dev * band, 128), jnp.float32)],
        name="restore_patches",
    )(order, back)
    return (restored.reshape(rows_dev, band, cells), spread[None])


def solution(mesh):
    placed = (
        P("mem", "band", None),
        P(),
        P("band", None),
        P("band", None, None),
        P("band", "mem"),
        P("band", "mem", None),
        P("band", "mem", None),
    )
    return jax.shard_map(
        local,
        mesh=mesh,
        in_specs=placed,
        out_specs=(P("mem", "band", None), P("band", "mem", None, None)),
        check_vma=False,
    )
```

```python
import functools
import math

import jax
import jax.numpy as jnp
from jax import lax
from jax.experimental import pallas as pl
from jax.experimental.pallas import tpu as pltpu
from jax.sharding import PartitionSpec as P

ITERS = 12
LIGHT = 8
MESH = pl.DeviceIdType.MESH
HIGHEST = lax.Precision.HIGHEST


def whole():
    return pl.BlockSpec(memory_space=pltpu.VMEM)


def pieces(x):
    high = x.astype(jnp.bfloat16)
    return high, (x - high.astype(jnp.float32)).astype(jnp.bfloat16)


def product(left, right, full, right_dim=0):
    lh, ll = left
    rh, rl = right
    lefts = [lh, lh, ll, ll] if full else [lh, lh, ll]
    rights = [rh, rl, rh, rl] if full else [rh, rl, rh]
    return lax.dot_general(
        jnp.concatenate(lefts, axis=1),
        jnp.concatenate(rights, axis=right_dim),
        (((1,), (right_dim,)), ((), ())),
        preferred_element_type=jnp.float32,
    )


def exact(left, right, right_dim=0):
    return lax.dot_general(
        left, right, (((1,), (right_dim,)), ((), ())),
        precision=HIGHEST, preferred_element_type=jnp.float32,
    )


def sweep(y_ref, z_ref, group, full, last):
    for g in range(group):
        y, z = y_ref[g], z_ref[g]
        yp, zp = pieces(y), pieces(z)
        turn = pieces(product(zp, yp, full))
        if not last:
            y_ref[g] = 1.5 * y - 0.5 * product(yp, turn, full)
        z_ref[g] = 1.5 * z - 0.5 * product(turn, zp, full)


def analyse(n_mem, group, order_ref, count_ref, x_ref, op_ref, index_ref, value_ref, weight_ref, spread_ref, back_ref,
            lanes_ref, sends_ref, inbox, outbox, pert_ref, y_ref, z_ref, col_ref, mean_ref, in_send, in_recv, own_sem, out_send, out_recv, home_sem):
    per_worker, workers, rows_dev, cells = inbox.shape
    members = workers * rows_dev
    levels = op_ref.shape[0]
    slots = index_ref.shape[1]
    me = lax.axis_index("mem")

    def greet(d, carry):
        pl.semaphore_signal(barrier, inc=1, device_id={"mem": lax.rem(me + d, n_mem)}, device_id_type=MESH)
        return carry

    barrier = pltpu.get_barrier_semaphore()
    lax.fori_loop(1, n_mem, greet, 0)
    halves, _, lanes = lanes_ref.shape
    band = order_ref.shape[0]
    for h in range(halves):
        lanes_ref[h] = x_ref[:, h * lanes:(h + 1) * lanes]

    def stage(i):
        def one(w, carry):
            q = order_ref[w * per_worker + i]
            for h in range(halves):
                sends_ref[w, i, :, h * lanes:(h + 1) * lanes] = lanes_ref[h, pl.ds(q, rows_dev, stride=band), :]
            return carry

        lax.fori_loop(0, n_mem, one, 0)

    stage(0)
    pl.semaphore_wait(barrier, n_mem - 1)

    def own_in(i):
        return pltpu.make_async_copy(sends_ref.at[me, i], inbox.at[i, me], own_sem.at[i])

    def own_back(i):
        return pltpu.make_async_copy(outbox.at[i, me], back_ref.at[me, i], home_sem.at[i])

    def issue(i):
        own_in(i).start()

        def one(d, carry):
            peer = lax.rem(me + d, n_mem)
            pltpu.make_async_remote_copy(
                src_ref=sends_ref.at[peer, i], dst_ref=inbox.at[i, me],
                send_sem=in_send, recv_sem=in_recv.at[i],
                device_id={"mem": peer}, device_id_type=MESH,
            ).start()
            return carry

        lax.fori_loop(1, n_mem, one, 0)

    def feed(i, carry):
        stage(i + 1)
        issue(i)
        return carry

    lax.fori_loop(0, per_worker - 1, feed, 0)
    issue(per_worker - 1)
    eye = (
        lax.broadcasted_iota(jnp.int32, (members, members), 0)
        == lax.broadcasted_iota(jnp.int32, (members, members), 1)
    )

    def run(base, size):
        for g in range(size):
            own_in(base + g).wait()
            arrived = inbox.at[base + g, pl.ds(0, n_mem - 1)]
            pltpu.make_async_copy(arrived, arrived, in_recv.at[base + g]).wait()
        scales = [prepare(base + g, g) for g in range(size)]

        def light(k, carry):
            sweep(y_ref, z_ref, size, False, False)
            return carry

        def firm(k, carry):
            sweep(y_ref, z_ref, size, True, False)
            return carry

        lax.fori_loop(1, LIGHT, light, 0)
        lax.fori_loop(LIGHT, ITERS - 1, firm, 0)
        sweep(y_ref, z_ref, size, True, True)
        for g in range(size):
            finish(base + g, g, scales[g])
            launch(base + g)

    def launch(spot):
        own_back(spot).start()

        def one(d, carry):
            peer = lax.rem(me + d, n_mem)
            pltpu.make_async_remote_copy(
                src_ref=outbox.at[spot, peer], dst_ref=back_ref.at[me, spot],
                send_sem=out_send, recv_sem=out_recv,
                device_id={"mem": peer}, device_id_type=MESH,
            ).start()
            return carry

        lax.fori_loop(1, n_mem, one, 0)

    def prepare(spot, g):
        state = inbox[spot].reshape(members, cells)
        mean = jnp.mean(state, axis=0, keepdims=True)
        pert = state - mean
        pert_ref[g] = pert
        op = op_ref[...]
        columns = cells // levels
        op_pieces = pieces(op)
        chan = jnp.concatenate([product(pieces(pert[:, c * levels:(c + 1) * levels]), op_pieces, False) for c in range(columns)], axis=1)
        wide = jnp.broadcast_to(mean, (8, cells))
        chan_mean = jnp.concatenate([exact(wide[:, c * levels:(c + 1) * levels], op) for c in range(columns)], axis=1)
        width = chan.shape[1]
        index = index_ref[pl.ds(me * per_worker + spot, 1), :]
        live = lax.broadcasted_iota(jnp.int32, (1, slots), 1) < count_ref[spot]
        weight = jnp.where(live, weight_ref[pl.ds(spot, 1), :], 0.0)
        value = weight * value_ref[pl.ds(spot, 1), :]
        picker = (lax.broadcasted_iota(jnp.int32, (width, slots), 0) == index).astype(jnp.bfloat16)
        sub = lax.broadcasted_iota(jnp.int32, (16, slots), 0)
        stack = jnp.where(sub == 0, weight, jnp.where(sub == 1, value, 0.0))
        s0 = stack.astype(jnp.bfloat16)
        left = stack - s0.astype(jnp.float32)
        s1 = left.astype(jnp.bfloat16)
        s2 = (left - s1.astype(jnp.float32)).astype(jnp.bfloat16)
        binned = lax.dot_general(
            jnp.concatenate([s0, s1, s2], axis=0), picker, (((1,), (1,)), ((), ())),
            preferred_element_type=jnp.float32,
        )
        binned = binned[0:16] + (binned[16:32] + binned[32:48])
        total = binned[0:1]
        innov = binned[1:2] - chan_mean[0:1] * total
        system = exact(chan * total, chan, 1) + jnp.where(eye, members - 1.0, 0.0)
        col_ref[g] = jnp.sum(chan * innov, axis=1, keepdims=True)
        mean_ref[g] = wide
        trace_value = jnp.sum(jnp.sum(jnp.where(eye, system, 0.0), axis=0, keepdims=True), axis=1, keepdims=True)
        y = system / trace_value
        yp = pieces(y)
        z_ref[g] = jnp.where(eye, 1.5, 0.0) - 0.5 * y
        y_ref[g] = 1.5 * y - 0.5 * product(yp, yp, False)
        return trace_value

    def finish(spot, g, trace_value):
        z = z_ref[g]
        spread = z * (math.sqrt(members - 1.0) / jnp.sqrt(trace_value))
        spread_ref[spot] = spread
        inner = jnp.sum(z * col_ref[g], axis=0, keepdims=True)
        weights = jnp.sum(z * inner, axis=1, keepdims=True) / trace_value
        pert = pert_ref[g]
        shift = mean_ref[g][0:1] + jnp.sum(pert * weights, axis=0, keepdims=True)
        update = shift + product(pieces(spread), pieces(pert), False)
        outbox[spot] = update.reshape(workers, rows_dev, cells)

    edge = 1 if group > 1 and per_worker % group == 0 and per_worker > group else 0
    middle = (per_worker - 2 * edge) // group

    def step(t, carry):
        run(edge + t * group, group)
        return carry

    if edge:
        run(0, 1)
    lax.fori_loop(0, middle, step, 0)
    if edge:
        run(per_worker - 1, 1)
    sent = sends_ref.at[pl.ds(0, n_mem - 1)]
    pltpu.make_async_copy(sent, sent, in_send).wait()
    posted = back_ref.at[pl.ds(0, n_mem - 1)]
    pltpu.make_async_copy(posted, posted, out_send).wait()
    pltpu.make_async_copy(posted, posted, out_recv).wait()
    for i in range(per_worker):
        own_back(i).wait()


def scatter_kernel(n_mem, order_ref, *refs):
    ins, out, lanes_ref = refs[:-2], refs[-2], refs[-1]
    halves, _, lanes = lanes_ref.shape
    band = order_ref.shape[0]
    per = ins[0].shape[1]
    rows = ins[0].shape[2]
    chunks = len(ins)
    for c, block in enumerate(ins):
        @pl.loop(0, n_mem * per, unroll=8)
        def _(t):
            w, i = t // per, lax.rem(t, per)
            q = order_ref[(w * chunks + c) * per + i]
            for h in range(halves):
                lanes_ref[h, pl.ds(q, rows, stride=band), :] = block[w, i, :, h * lanes:(h + 1) * lanes]

    for h in range(halves):
        out[:, h * lanes:(h + 1) * lanes] = lanes_ref[h]


def local(ensemble, column_operator, patch_order, obs_index, obs_count, obs_values, obs_precision):
    rows_dev, band, cells = ensemble.shape
    slots = obs_index.shape[2]
    n_mem = lax.axis_size("mem")
    per_worker = band // n_mem
    members = rows_dev * n_mem
    group = 2 if per_worker % 2 == 0 else 1
    order = patch_order[0]
    smem = pl.BlockSpec(memory_space=pltpu.SMEM)
    block = jax.ShapeDtypeStruct((n_mem, per_worker, rows_dev, cells), jnp.float32)

    spread, back = pl.pallas_call(
        functools.partial(analyse, n_mem, group),
        out_shape=[jax.ShapeDtypeStruct((per_worker, members, members), jnp.float32), block],
        in_specs=[smem, smem, whole(), whole(), whole(), whole(), whole()],
        out_specs=[whole(), pl.BlockSpec(memory_space=pl.ANY)],
        scratch_shapes=[
            pltpu.VMEM((cells // 128, rows_dev * band, 128), jnp.float32),
            pltpu.VMEM((n_mem, per_worker, rows_dev, cells), jnp.float32),
            pltpu.VMEM((per_worker, n_mem, rows_dev, cells), jnp.float32),
            pltpu.VMEM((per_worker, n_mem, rows_dev, cells), jnp.float32),
            pltpu.VMEM((group, members, cells), jnp.float32),
            pltpu.VMEM((group, members, members), jnp.float32),
            pltpu.VMEM((group, members, members), jnp.float32),
            pltpu.VMEM((group, members, 1), jnp.float32),
            pltpu.VMEM((group, 8, cells), jnp.float32),
            pltpu.SemaphoreType.DMA(()),
            pltpu.SemaphoreType.DMA((per_worker,)),
            pltpu.SemaphoreType.DMA((per_worker,)),
            pltpu.SemaphoreType.DMA(()),
            pltpu.SemaphoreType.DMA(()),
            pltpu.SemaphoreType.DMA((per_worker,)),
        ],
        compiler_params=pltpu.CompilerParams(collective_id=0, has_side_effects=True),
        name="analyse",
    )(order, obs_count[0], ensemble.reshape(rows_dev * band, cells), column_operator, obs_index[0], obs_values[0], obs_precision[0])

    restored = pl.pallas_call(
        functools.partial(scatter_kernel, n_mem),
        out_shape=jax.ShapeDtypeStruct((rows_dev * band, cells), jnp.float32),
        in_specs=[smem] + [whole()],
        out_specs=whole(),
        scratch_shapes=[pltpu.VMEM((cells // 128, rows_dev * band, 128), jnp.float32)],
        name="restore_patches",
    )(order, back)
    return (restored.reshape(rows_dev, band, cells), spread[None])


def solution(mesh):
    placed = (
        P("mem", "band", None),
        P(),
        P("band", None),
        P("band", None, None),
        P("band", "mem"),
        P("band", "mem", None),
        P("band", "mem", None),
    )
    return jax.shard_map(
        local,
        mesh=mesh,
        in_specs=placed,
        out_specs=(P("mem", "band", None), P("band", "mem", None, None)),
        check_vma=False,
    )
```
